32 devices in a mesh: section: 2 (over core), req: 4 (over z), head: 4 (over y, x).
Axes of the slice: x: 2, y: 2, z: 4, core: 2. Of those that a mesh axis runs over, the one named last changes fastest.
Arguments:
- tokens: bfloat16 [128, 1024], P('req'), may hold values from -60 to 60, as said below
- deal: int32 [128], P('req'), may hold values from 0 to 127, each once
- lengths: int32 [2, 128], P('section', 'req'), may hold values from 2 to 256, as said below
- cache_keys: bfloat16 [2, 128, 256, 1024], P('section', 'req', None, 'head'), may hold values from -1024 to 1024
- cache_values: bfloat16 [2, 128, 256, 1024], P('section', 'req', None, 'head'), may hold values from -6 to 6
- w_qkv: bfloat16 [2, 1024, 3, 1024], P('section', None, None, 'head'), may hold values from -0.1875 to 0.1875
- w_out: bfloat16 [2, 1024, 1024], P('section', 'head'), may hold values from -0.1875 to 0.1875
- attn_gain: float32 [2, 1024], P('section'), may hold values from 0.5 to 1.5
- ffn_gain: float32 [2, 1024], P('section'), may hold values from 0.5 to 1.5
- w_gate: bfloat16 [2, 1024, 45056], P('section', None, ('req', 'head')), may hold values from -0.1875 to 0.1875
- w_up: bfloat16 [2, 1024, 45056], P('section', None, ('req', 'head')), may hold values from -0.1875 to 0.1875
- w_down: bfloat16 [2, 45056, 1024], P('section', ('req', 'head')), may hold values from -0.109375 to 0.109375
- routes: int32 [2, 128, 2], P('section', 'req'), may hold values from 0 to 15, all different within a row; in each aligned block of 16 rows (0 to 15, 16 to 31, ..., all dimensions but the last counted through in order) at most 4 rows name the same one
- gates: bfloat16 [2, 128, 2], P('section', 'req'), may hold values from 0.25 to 1
Outputs:
- layer_out: bfloat16 [2, 128, 1024], P('section', 'req')
The draws below stay inside these ranges and needn't reach their ends.
Inputs may be any that keep to these rules, and one draw needn't show every extreme that they name: `tokens`: hidden states with row and feature scales that differ. `deal`: each of 0 to 127 appears once. `lengths`: in each layer, one of the 32 slots of each index of req holds a length of exactly 256; the others are anywhere from 2 to 256. `routes`: the two experts of a slot differ; in each aligned block of 16 slots of one layer no expert is named more than 4 times.
All inputs are finite; a program needn't handle non-finite values.
Results may differ from the reference program's by a relative error of at most 0.0053.
Values may be sent and summed in bfloat16 or wider, within the bound.
A program may use at most 128 MiB of HBM per device.

```python
import math
import jax
import jax.numpy as jnp
import numpy as np
from jax import lax

D = 1024
HEADS = 16
HEAD_DIM = 64
EXPERTS = 16
FF = 2816
REQ_DEV = 32
CONTEXT = 256
REQS = 128
BLOCK_ROWS = 16
CAPACITY = 4
N_SECTION = 2


def draw_tokens(key, part):
    key_a, key_b, key_c = jax.random.split(key, 3)
    values = jnp.clip(jax.random.normal(key_a, (REQS, D), jnp.float32), -6.0, 6.0)
    row_scale = jnp.exp(jax.random.uniform(key_b, (REQS, 1), jnp.float32, 0.0, 2.302585))
    col_scale = jnp.exp(jax.random.uniform(key_c, (1, D), jnp.float32, 0.0, 2.302585))
    return (values * row_scale * col_scale * 0.1).astype(jnp.bfloat16)


def draw_lengths(key, part):
    key_a, key_b = jax.random.split(key)
    uniform_lengths = jax.random.randint(key_a, (N_SECTION, REQS), 2, CONTEXT + 1)
    longest = jax.random.randint(key_b, (N_SECTION, REQS // REQ_DEV, 1), 0, REQ_DEV)
    offsets = jnp.arange(REQ_DEV).reshape(1, 1, REQ_DEV)
    marked = (offsets == longest).reshape(N_SECTION, REQS)
    return jnp.where(marked, CONTEXT, uniform_lengths).astype(jnp.int32)


def draw_cache_keys(key, part):
    key_a = jax.random.fold_in(key, 0)
    full_shape = (N_SECTION, REQS, CONTEXT, HEADS * HEAD_DIM)
    values = jnp.clip(jax.random.normal(key_a, full_shape, jnp.float32), -6.0, 6.0)
    return jnp.clip(values, -1024.0, 1024.0).astype(jnp.bfloat16)


def block_scale(rng, dims, cuts, low, top_value):
    gain, own = 1.0, jax.random.fold_in(rng, 6)
    for axis_at, shards_of in cuts:
        steps = jnp.exp(jax.random.uniform(jax.random.fold_in(own, axis_at), (shards_of,), jnp.float32, low / len(cuts), top_value / len(cuts)))
        gain = gain * jnp.repeat(steps, dims[axis_at] // shards_of).reshape([-1 if axis == axis_at else 1 for axis in range(len(dims))])
    return gain


def assign_block(own_key, own, number, rows, count, top, most, lean):
    sequence = jax.random.permutation(own_key, count)
    crowded, ordinary = load_shares(count, rows * top, most, lean, True), load_shares(count, rows * top, most, lean, False)
    places = jnp.arange(count)

    def named(sizes, offset_by):
        used = int((sizes > 0).sum())
        fixed = max(1, used // 4)
        passed = fixed + (places - fixed + offset_by * (used - fixed)) % max(1, count - fixed)
        return jnp.zeros((count,), jnp.int32).at[sequence[jnp.where(places < fixed, places, passed)]].set(jnp.asarray(sizes, jnp.int32))

    sizes = jnp.where(number % 4 == 0, named(crowded, number // 4), named(ordinary, number - number // 4 - 1))
    mixed = jax.random.permutation(jax.random.fold_in(own, 3), count)
    source_of, receiver = mixed[0:count // 2 * 2:2], mixed[1:count // 2 * 2:2]
    room = jnp.minimum(sizes[source_of] - 1, most - sizes[receiver]) // 2
    room = jnp.where((source_of == sequence[0]) | (receiver == sequence[0]) | (sizes[receiver] == 0), 0, jnp.maximum(room, 0))
    passed = jax.random.randint(jax.random.fold_in(own, 4), (count // 2,), 0, 1 << 20) % (room + 1)
    sizes = sizes.at[source_of].add(-passed).at[receiver].add(passed)
    items = jnp.searchsorted(jnp.cumsum(sizes), jnp.arange(rows * top), side="right").astype(jnp.int32)
    table = items.reshape(top, rows).T
    table = table[jax.random.permutation(jax.random.fold_in(own, 1), rows)]
    offset_by = jax.random.randint(jax.random.fold_in(own, 2), (rows, 1), 0, top)
    return jnp.take_along_axis(table, (jnp.arange(top)[None, :] + offset_by) % top, axis=1)


def load_shares(amount, total, bound, slope, full):
    weights = [(1 << 20) // math.isqrt(standing ** slope) + 1 for standing in range(1, amount + 1)]
    largest = bound if full else min(bound, max(-(-total // amount), total * weights[0] // sum(weights)))
    least = 1 if total - largest >= amount - 1 else 0
    given, spare = [largest] + [least] * (amount - 1), total - largest - least * (amount - 1)
    while spare > 0:
        free = [i for i in range(1, amount) if given[i] < largest] or [i for i in range(1, amount) if given[i] < bound]
        whole, budget = sum([weights[i] for i in free]), spare
        for i in free:
            extra = min(bound - given[i], max(1, budget * weights[i] // whole), spare)
            given[i] = given[i] + extra
            spare = spare - extra
    return np.array(given)


def bell_draw(key, dims, spread, bound, shards=(), kind=jnp.bfloat16):
    values = jax.random.normal(key, dims, jnp.float32) * spread
    if len(shards) > 0:
        values = block_scale(key, dims, shards, -0.22, 0.18) * values
    return jnp.clip(values, min=-bound, max=bound).astype(kind)


def setup_inputs(seed: int = 0) -> dict:
    key_list = jax.random.split(jax.random.key(seed), 15)
    tokens = draw_tokens(jax.random.fold_in(key_list[14], 71), 0)
    deal = jax.random.permutation(key_list[1], REQS).astype(jnp.int32)
    lengths = draw_lengths(jax.random.fold_in(key_list[14], 71), 0)
    cache_keys = draw_cache_keys(jax.random.fold_in(key_list[14], 71), 0)
    cache_values = bell_draw(key_list[4], (N_SECTION, REQS, CONTEXT, HEADS * HEAD_DIM), 1.0, 6.0, ((0, 2), (1, 4), (3, 4)))
    w_qkv = bell_draw(key_list[5], (N_SECTION, D, 3, HEADS * HEAD_DIM), D ** -0.5, 0.1875, ((0, 2), (3, 4)))
    w_out = bell_draw(key_list[6], (N_SECTION, HEADS * HEAD_DIM, D), (HEADS * HEAD_DIM) ** -0.5, 0.1875, ((0, 2), (1, 4)))
    attn_gain = jnp.clip(0.5 + 1.0 * jax.random.uniform(key_list[7], (N_SECTION, D), jnp.float32) ** block_scale(key_list[7], (N_SECTION, D), ((0, 2),), -0.2, 0.2), 0.5, 1.5)
    ffn_gain = jnp.clip(0.5 + 1.0 * jax.random.uniform(key_list[8], (N_SECTION, D), jnp.float32) ** block_scale(key_list[8], (N_SECTION, D), ((0, 2),), -0.2, 0.2), 0.5, 1.5)
    w_gate = bell_draw(key_list[9], (N_SECTION, D, EXPERTS * FF), D ** -0.5, 0.1875, ((0, 2), (2, 16)))
    w_up = bell_draw(key_list[10], (N_SECTION, D, EXPERTS * FF), D ** -0.5, 0.1875, ((0, 2), (2, 16)))
    w_down = bell_draw(key_list[11], (N_SECTION, EXPERTS * FF, D), FF ** -0.5, 0.109375, ((0, 2), (1, 16)))
    routes_keys = jax.random.split(jax.random.fold_in(key_list[12], 1), N_SECTION * REQS // BLOCK_ROWS)
    routes_turns = jax.random.permutation(jax.random.fold_in(key_list[12], 3), N_SECTION * REQS // BLOCK_ROWS)
    routes = jax.vmap(lambda own, number: assign_block(jax.random.fold_in(key_list[12], 2), own, number, BLOCK_ROWS, EXPERTS, 2, CAPACITY, 2))(routes_keys, routes_turns).reshape((N_SECTION, REQS, 2))
    gates = jnp.clip(0.25 + 0.75 * jax.random.uniform(key_list[13], (N_SECTION, REQS, 2), jnp.float32) ** block_scale(key_list[13], (N_SECTION, REQS, 2), ((0, 2), (1, 4)), -0.2, 0.2), 0.25, 1.0).astype(jnp.bfloat16)
    return {"tokens": tokens, "deal": deal, "lengths": lengths, "cache_keys": cache_keys, "cache_values": cache_values, "w_qkv": w_qkv, "w_out": w_out, "attn_gain": attn_gain, "ffn_gain": ffn_gain, "w_gate": w_gate, "w_up": w_up, "w_down": w_down, "routes": routes, "gates": gates}


epsilon = 1e-06

def rms_scale(values, gain_row):
    mean_square = lax.optimization_barrier(jnp.mean(values * values, axis=-1, keepdims=True))
    return values * lax.rsqrt(mean_square + epsilon) * gain_row

def attend_block(arguments):
    queries, new_keys, new_values, key_cache, value_cache, lengths = arguments
    score_scale = 1.0 / math.sqrt(HEAD_DIM)
    scores = jnp.einsum('bhd,bjhd->bhj', queries.astype(jnp.float32), key_cache.astype(jnp.float32)) * score_scale
    own_score = lax.optimization_barrier(jnp.sum(queries.astype(jnp.float32) * new_keys.astype(jnp.float32), axis=-1)) * score_scale
    positions = jnp.arange(CONTEXT).astype(jnp.int32)
    in_range = positions[None, None, :] < lengths.astype(jnp.int32)[:, None, None]
    scores = jnp.where(in_range, scores, -jnp.inf)
    peak_score = jnp.maximum(lax.optimization_barrier(jnp.max(scores, axis=-1)), own_score)
    cache_weight = jnp.exp(scores - peak_score[..., None])
    own_weight = jnp.exp(own_score - peak_score)
    denominator = lax.optimization_barrier(jnp.sum(cache_weight, axis=-1)) + own_weight
    cache_prob = (cache_weight / denominator[..., None]).astype(jnp.bfloat16)
    own_prob = (own_weight / denominator).astype(jnp.bfloat16)
    attended = jnp.einsum('bhj,bjhd->bhd', cache_prob.astype(jnp.float32), value_cache.astype(jnp.float32))
    attended = attended + own_prob.astype(jnp.float32)[..., None] * new_values.astype(jnp.float32)
    return attended.astype(jnp.bfloat16)

def run_layer(stream, lengths, key_cache, value_cache, qkv_weight, out_weight, attn_gain, ffn_gain, gate_weight, up_weight, down_weight, route_ids, gate_values):
    row_count = stream.shape[0]
    head_cols = HEADS * HEAD_DIM
    normed = rms_scale(stream.astype(jnp.float32), attn_gain).astype(jnp.bfloat16)
    projected = jnp.dot(normed, qkv_weight.reshape(D, 3 * head_cols), preferred_element_type=jnp.float32).astype(jnp.bfloat16)
    queries = projected[:, :head_cols].reshape(row_count, HEADS, HEAD_DIM)
    new_keys = projected[:, head_cols:2 * head_cols].reshape(row_count, HEADS, HEAD_DIM)
    new_values = projected[:, 2 * head_cols:].reshape(row_count, HEADS, HEAD_DIM)
    group_count = row_count // REQ_DEV

    def grouped(tensor):
        return tensor.reshape((group_count, REQ_DEV) + tensor.shape[1:])
    attended = lax.map(attend_block, (grouped(queries), grouped(new_keys), grouped(new_values), grouped(key_cache.reshape(row_count, CONTEXT, HEADS, HEAD_DIM)), grouped(value_cache.reshape(row_count, CONTEXT, HEADS, HEAD_DIM)), grouped(lengths)))
    attended = attended.reshape(row_count, head_cols)
    residual = stream.astype(jnp.float32) + jnp.dot(attended, out_weight, preferred_element_type=jnp.float32)
    normed_ffn = rms_scale(residual, ffn_gain).astype(jnp.bfloat16)
    row_limit = CAPACITY * (REQS // BLOCK_ROWS)
    mixture = jnp.zeros((row_count, D), jnp.float32)
    for expert in range(EXPERTS):
        matched = route_ids == expert
        weight = lax.optimization_barrier(jnp.sum(jnp.where(matched, gate_values.astype(jnp.float32), 0.0), axis=1))
        picked = jnp.nonzero(jnp.any(matched, axis=1), size=row_limit, fill_value=row_count)[0].astype(jnp.int32)
        safe_index = jnp.minimum(picked, row_count - 1).astype(jnp.int32)
        chosen_rows = normed_ffn[safe_index]
        row_weight = jnp.where(picked < row_count, weight[safe_index], 0.0)
        gate_part = jnp.dot(chosen_rows, gate_weight[:, expert * FF:(expert + 1) * FF], preferred_element_type=jnp.float32)
        up_part = jnp.dot(chosen_rows, up_weight[:, expert * FF:(expert + 1) * FF], preferred_element_type=jnp.float32)
        hidden = (row_weight[:, None] * jax.nn.gelu(gate_part, approximate=True) * up_part).astype(jnp.bfloat16)
        partial_terms = jnp.dot(hidden, down_weight[expert * FF:(expert + 1) * FF], preferred_element_type=jnp.float32)
        mixture = mixture.at[picked].add(partial_terms, mode='drop')
    return (residual + mixture).astype(jnp.bfloat16)

def reference(tokens, deal, lengths, cache_keys, cache_values, w_qkv, w_out, attn_gain, ffn_gain, w_gate, w_up, w_down, routes, gates):
    stream = tokens[deal]
    outputs = []
    for layer_index in range(N_SECTION):
        stream = run_layer(stream, lengths[layer_index], cache_keys[layer_index], cache_values[layer_index], w_qkv[layer_index], w_out[layer_index], attn_gain[layer_index], ffn_gain[layer_index], w_gate[layer_index], w_up[layer_index], w_down[layer_index], routes[layer_index], gates[layer_index])
        outputs.append(jnp.zeros_like(stream).at[deal].set(stream))
    return jnp.stack(outputs)
```

```python
import functools
import math

import jax
import jax.numpy as jnp
from jax import lax
from jax.experimental import pallas as pl
from jax.experimental.pallas import tpu as pltpu
from jax.sharding import PartitionSpec as P

HEAD_DIM = 64
EXPERTS = 16
FF = 2816
LANES = 128
DEAL_LANE = EXPERTS
LENGTH_LANE = EXPERTS + 1
HEAD_ROWS = 16
MESH = pl.DeviceIdType.MESH


epsilon = 1e-06


def rms_scale(values, gain_row):
    mean_square = jnp.mean(values * values, axis=-1, keepdims=True)
    return values * lax.rsqrt(mean_square + epsilon) * gain_row


def gelu(v):
    return 0.5 * v * (1.0 + jnp.tanh(math.sqrt(2.0 / math.pi) * (v + 0.044715 * (v * v * v))))


def batched(a, b, dims):
    return lax.dot_general(a, b, (dims, ((0,), (0,))), preferred_element_type=jnp.float32)


def attend(proj, lengths, key_cache, value_cache):
    slots, context, cols = key_cache.shape
    score_scale = 1.0 / math.sqrt(HEAD_DIM)
    queries = proj[:, :cols][:, None, :]
    new_keys = proj[:, cols : 2 * cols][:, None, :]
    new_values = proj[:, 2 * cols :][:, None, :]
    row_at = lax.broadcasted_iota(jnp.int32, (1, HEAD_ROWS, cols), 1)
    lane_at = lax.broadcasted_iota(jnp.int32, (1, HEAD_ROWS, cols), 2)
    head_mask = (lane_at // HEAD_DIM == row_at).astype(jnp.float32)
    spread = queries * head_mask
    scores = batched(spread.astype(jnp.bfloat16), key_cache[...], ((2,), (2,))) * score_scale
    own_score = jnp.sum(spread * new_keys, axis=-1, keepdims=True) * score_scale
    positions = lax.broadcasted_iota(jnp.int32, (slots, HEAD_ROWS, context), 2).astype(jnp.float32)
    limit = jnp.broadcast_to(lengths, (slots, context))[:, None, :]
    scores = jnp.where(positions < limit, scores, -jnp.inf)
    peak = jnp.maximum(jnp.max(scores, axis=-1, keepdims=True), own_score)
    cache_weight = jnp.exp(scores - peak)
    own_weight = jnp.exp(own_score - peak)
    denominator = jnp.sum(cache_weight, axis=-1, keepdims=True) + own_weight
    cache_prob = (cache_weight / denominator).astype(jnp.bfloat16)
    own_prob = (own_weight / denominator).astype(jnp.bfloat16).astype(jnp.float32)
    attended = batched(cache_prob, value_cache[...], ((2,), (1,))) + own_prob * new_values
    return jnp.sum(attended * head_mask, axis=1).astype(jnp.bfloat16)


def kernel(
    req_count,
    head_count,
    meta_ref,
    tok_ref,
    again_ref,
    fgain_ref,
    wqkv_hbm,
    key_hbm,
    value_hbm,
    wout_hbm,
    wgate_hbm,
    wup_hbm,
    wdown_hbm,
    out_ref,
    wqkv,
    key_cache,
    value_cache,
    wout,
    wgate,
    wup,
    wdown,
    meta_all,
    tok_all,
    stream_in,
    stream,
    part_out,
    part_in,
    rows_all,
    rows_flat,
    total,
    terms_out,
    terms_in,
    made,
    load_sem,
    meta_sem,
    tok_sem,
    next_sem,
    head_sem,
    rows_sem,
    terms_sem,
    made_sem,
):
    sec = lax.axis_index("section")
    req = lax.axis_index("req")
    head = lax.axis_index("head")
    count = req_count * head_count
    me = req * head_count + head
    slots, width = tok_ref.shape
    own_rows = slots // head_count
    reqs = slots * req_count
    units = wgate.shape[1]
    chunk = 256 if units % 256 == 0 else units

    loads = [
        pltpu.make_async_copy(src.at[0], dst, load_sem.at[i])
        for i, (src, dst) in enumerate(
            [
                (key_hbm, key_cache),
                (value_hbm, value_cache),
                (wout_hbm, wout),
                (wgate_hbm, wgate),
                (wup_hbm, wup),
                (wdown_hbm, wdown),
            ]
        )
    ]
    load_qkv = pltpu.make_async_copy(wqkv_hbm, wqkv, load_sem.at[6])
    load_qkv.start()
    for load in loads:
        load.start()

    def peer_of(k):
        peer = lax.rem(me + k, count)
        return peer, (sec, peer // head_count, lax.rem(peer, head_count))

    def req_peer(k):
        return (sec, lax.rem(req + k, req_count), head)

    def head_peer(k):
        other = lax.rem(head + k, head_count)
        return other, (sec, req, other)

    def each(first, last, body):
        def step(k, carry):
            body(k)
            return carry

        lax.fori_loop(first, last, step, 0)

    barrier = pltpu.get_barrier_semaphore()

    def greet(k):
        _, target = peer_of(k)
        pl.semaphore_signal(barrier, inc=1, device_id=target, device_id_type=MESH)

    def greet_other(k):
        pl.semaphore_signal(barrier, inc=1, device_id=(1 - sec, req, k), device_id_type=MESH)

    each(1, count, greet)
    each(0, head_count, greet_other)
    pl.semaphore_wait(barrier, count - 1 + head_count)

    def remote(src, dst, sems, k, target):
        return pltpu.make_async_remote_copy(
            src_ref=src,
            dst_ref=dst,
            send_sem=sems.at[0, k],
            recv_sem=sems.at[1, k],
            device_id=target,
            device_id_type=MESH,
        )

    def meta_copy(k):
        return remote(meta_ref, meta_all.at[req], meta_sem, k, req_peer(k))

    def tok_copy(k):
        return remote(tok_ref, tok_all.at[req], tok_sem, k, req_peer(k))

    def next_copy(k):
        return pltpu.make_async_remote_copy(
            src_ref=made.at[me],
            dst_ref=stream_in.at[head],
            send_sem=next_sem.at[0, k],
            recv_sem=next_sem.at[1, head],
            device_id=(1, req, k),
            device_id_type=MESH,
        )

    def next_arrival(k):
        return pltpu.make_async_remote_copy(
            src_ref=made.at[me],
            dst_ref=stream_in.at[k],
            send_sem=next_sem.at[0, k],
            recv_sem=next_sem.at[1, k],
            device_id=(0, req, k),
            device_id_type=MESH,
        )

    def head_copy(k):
        other, target = head_peer(k)
        return remote(part_out.at[other], part_in.at[head], head_sem, k, target)

    def rows_copy(k):
        _, target = peer_of(k)
        return remote(rows_all.at[me], rows_all.at[me], rows_sem, k, target)

    def terms_copy(k):
        peer, target = peer_of(k)
        return remote(terms_out.at[peer], terms_in.at[me], terms_sem, k, target)

    def made_copy(k):
        _, target = peer_of(k)
        return remote(made.at[me], made.at[me], made_sem, k, target)

    @pl.when(sec == 0)
    def _():
        each(1, req_count, lambda k: tok_copy(k).start())

    each(1, req_count, lambda k: meta_copy(k).start())
    meta_all[req] = meta_ref[...]

    @pl.when(sec == 0)
    def _():
        tok_all[req] = tok_ref[...]
        each(1, req_count, lambda k: tok_copy(k).wait())
        deal = meta_ref[:, DEAL_LANE : DEAL_LANE + 1].astype(jnp.int32)
        taken = lax.broadcasted_iota(jnp.int32, (slots, reqs), 1) == deal
        dealt = jnp.dot(
            taken.astype(jnp.float32).astype(jnp.bfloat16),
            tok_all[...].reshape(reqs, width),
            preferred_element_type=jnp.float32,
        )
        stream[...] = dealt.reshape(head_count, own_rows, width)

    @pl.when(sec == 1)
    def _():
        each(0, head_count, lambda k: next_arrival(k).wait_recv())
        stream[...] = stream_in[...].astype(jnp.float32)

    normed = rms_scale(stream[...].reshape(slots, width), again_ref[...]).astype(jnp.bfloat16)
    load_qkv.wait()
    proj = jnp.dot(normed, wqkv[...], preferred_element_type=jnp.float32)
    proj = proj.astype(jnp.bfloat16).astype(jnp.float32)
    for load in loads[:3]:
        load.wait()
    attended = attend(
        proj, meta_ref[:, LENGTH_LANE : LENGTH_LANE + 1], key_cache, value_cache
    )
    partial_value = jnp.dot(attended, wout[...], preferred_element_type=jnp.float32)
    part_out[...] = partial_value.reshape(head_count, own_rows, width)
    each(1, head_count, lambda k: head_copy(k).start())
    part_in[head] = part_out[head]
    each(1, head_count, lambda k: head_copy(k).wait())
    residual = stream[head] + jnp.sum(part_in[...], axis=0)
    rows_all[me] = rms_scale(residual, fgain_ref[...]).astype(jnp.bfloat16)
    each(1, count, lambda k: rows_copy(k).start())
    each(1, req_count, lambda k: meta_copy(k).wait())
    total[...] = jnp.zeros_like(total)
    lane_at = lax.broadcasted_iota(jnp.int32, (reqs, LANES), 1)
    meta_rows = meta_all[...].reshape(reqs, LANES)
    row_weight = jnp.sum(
        jnp.where(lane_at == me * units // FF, meta_rows, 0.0), axis=1, keepdims=True
    )
    each(1, count, lambda k: rows_copy(k).wait())
    rows_flat[...] = (
        rows_all[...].astype(jnp.float32).reshape(reqs, width).astype(jnp.bfloat16)
    )
    for load in loads[3:]:
        load.wait()

    def expert(c):
        at = pl.ds(pl.multiple_of(c * chunk, chunk), chunk)
        rows = rows_flat[...]
        gate_part = jnp.dot(rows, wgate[:, at], preferred_element_type=jnp.float32)
        up_part = jnp.dot(rows, wup[:, at], preferred_element_type=jnp.float32)
        hidden = (row_weight * gelu(gate_part) * up_part).astype(jnp.bfloat16)
        total[...] += jnp.dot(hidden, wdown[at, :], preferred_element_type=jnp.float32)

    each(0, units // chunk, expert)
    terms_out[...] = total[...].reshape(count, own_rows, width).astype(jnp.bfloat16)
    each(1, count, lambda k: terms_copy(k).start())
    terms_in[me] = terms_out[me]
    each(1, count, lambda k: terms_copy(k).wait())
    mixture = jnp.sum(terms_in[...].astype(jnp.float32), axis=0)
    made[me] = (residual + mixture).astype(jnp.bfloat16)

    @pl.when(sec == 0)
    def _():
        each(0, head_count, lambda k: next_copy(k).start())

    each(1, count, lambda k: made_copy(k).start())
    each(1, count, lambda k: made_copy(k).wait())
    first = req * slots
    deal_all = meta_all[...].reshape(reqs, LANES)[:, DEAL_LANE : DEAL_LANE + 1].astype(jnp.int32)
    placed = deal_all == first + lax.broadcasted_iota(jnp.int32, (reqs, slots), 1)
    result = lax.dot_general(
        placed.astype(jnp.float32).astype(jnp.bfloat16),
        made[...].astype(jnp.float32).reshape(reqs, width).astype(jnp.bfloat16),
        (((0,), (0,)), ((), ())),
        preferred_element_type=jnp.float32,
    )
    out_ref[...] = result.astype(jnp.bfloat16)

    @pl.when(sec == 0)
    def _():
        each(0, head_count, lambda k: next_copy(k).wait_send())


def on_device(
    tokens,
    deal,
    lengths,
    cache_keys,
    cache_values,
    w_qkv,
    w_out,
    attn_gain,
    ffn_gain,
    w_gate,
    w_up,
    w_down,
    routes,
    gates,
):
    req_count = lax.axis_size("req")
    head_count = lax.axis_size("head")
    count = req_count * head_count
    slots, width = tokens.shape
    own_rows = slots // head_count
    reqs = slots * req_count
    units = w_gate.shape[2]
    cols = w_out.shape[1]
    context = cache_keys.shape[2]
    lanes = jnp.arange(LANES, dtype=jnp.int32)[None, :]
    gate_values = gates[0].astype(jnp.float32)
    meta = jnp.where(lanes == routes[0][:, 0:1], gate_values[:, 0:1], 0.0)
    meta = meta + jnp.where(lanes == routes[0][:, 1:2], gate_values[:, 1:2], 0.0)
    meta = jnp.where(lanes == DEAL_LANE, deal.astype(jnp.float32)[:, None], meta)
    meta = jnp.where(lanes == LENGTH_LANE, lengths[0].astype(jnp.float32)[:, None], meta)
    qkv_weight = w_qkv[0].reshape(width, 3 * cols)
    bf16, f32 = jnp.bfloat16, jnp.float32
    vmem = pl.BlockSpec(memory_space=pltpu.VMEM)
    anywhere = pl.BlockSpec(memory_space=pl.ANY)

    def sems(n):
        return pltpu.SemaphoreType.DMA((2, n))

    out = pl.pallas_call(
        functools.partial(kernel, req_count, head_count),
        out_shape=jax.ShapeDtypeStruct((slots, width), bf16),
        in_specs=[vmem] * 4 + [anywhere] * 7,
        out_specs=vmem,
        scratch_shapes=[
            pltpu.VMEM((width, 3 * cols), bf16),
            pltpu.VMEM((slots, context, cols), bf16),
            pltpu.VMEM((slots, context, cols), bf16),
            pltpu.VMEM((cols, width), bf16),
            pltpu.VMEM((width, units), bf16),
            pltpu.VMEM((width, units), bf16),
            pltpu.VMEM((units, width), bf16),
            pltpu.VMEM((req_count, slots, LANES), f32),
            pltpu.VMEM((req_count, slots, width), bf16),
            pltpu.VMEM((head_count, own_rows, width), bf16),
            pltpu.VMEM((head_count, own_rows, width), f32),
            pltpu.VMEM((head_count, own_rows, width), f32),
            pltpu.VMEM((head_count, own_rows, width), f32),
            pltpu.VMEM((count, own_rows, width), bf16),
            pltpu.VMEM((reqs, width), bf16),
            pltpu.VMEM((reqs, width), f32),
            pltpu.VMEM((count, own_rows, width), bf16),
            pltpu.VMEM((count, own_rows, width), bf16),
            pltpu.VMEM((count, own_rows, width), bf16),
            pltpu.SemaphoreType.DMA((7,)),
            sems(req_count),
            sems(req_count),
            sems(head_count),
            sems(head_count),
            sems(count),
            sems(count),
            sems(count),
        ],
        compiler_params=pltpu.CompilerParams(
            collective_id=0, has_side_effects=True, vmem_limit_bytes=56 * 1024 * 1024
        ),
    )(
        meta,
        tokens,
        attn_gain,
        ffn_gain,
        qkv_weight,
        cache_keys,
        cache_values,
        w_out,
        w_gate,
        w_up,
        w_down,
    )
    return out[None]


def solution(mesh):
    return jax.shard_map(
        on_device,
        mesh=mesh,
        in_specs=(
            P("req", None),
            P("req"),
            P("section", "req"),
            P("section", "req", None, "head"),
            P("section", "req", None, "head"),
            P("section", None, None, "head"),
            P("section", "head", None),
            P("section", None),
            P("section", None),
            P("section", None, ("req", "head")),
            P("section", None, ("req", "head")),
            P("section", ("req", "head"), None),
            P("section", "req", None),
            P("section", "req", None),
        ),
        out_specs=P("section", "req", None),
        check_vma=False,
    )
```

```python
import functools
import math

import jax
import jax.numpy as jnp
from jax import lax
from jax.experimental import pallas as pl
from jax.experimental.pallas import tpu as pltpu
from jax.sharding import PartitionSpec as P

HEAD_DIM = 64
EXPERTS = 16
FF = 2816
LANES = 128
DEAL_LANE = EXPERTS
HEAD_ROWS = 16
PARTS = 2
MESH = pl.DeviceIdType.MESH


epsilon = 1e-06


def rms_scale(values, gain_row):
    mean_square = jnp.mean(values * values, axis=-1, keepdims=True)
    return values * lax.rsqrt(mean_square + epsilon) * gain_row


def column(row):
    size = row.shape[1]
    diagonal = lax.broadcasted_iota(jnp.int32, (size, size), 0) == lax.broadcasted_iota(
        jnp.int32, (size, size), 1
    )
    return jnp.sum(jnp.where(diagonal, row, 0.0), axis=1, keepdims=True)


def gathered(chosen, values):
    return lax.dot_general(
        chosen.astype(jnp.bfloat16),
        values,
        (((0,), (0,)), ((), ())),
        preferred_element_type=jnp.float32,
    )


def flat(blocks):
    count, rows, width = blocks.shape
    return blocks[...].astype(jnp.float32).reshape(count * rows, width).astype(jnp.bfloat16)


def gelu(v):
    return 0.5 * v * (1.0 + jnp.tanh(math.sqrt(2.0 / math.pi) * (v + 0.044715 * (v * v * v))))


def batched(a, b, dims):
    return lax.dot_general(a, b, (dims, ((0,), (0,))), preferred_element_type=jnp.float32)


def attend(proj, lengths, key_cache, value_cache):
    slots, context, cols = key_cache.shape
    score_scale = 1.0 / math.sqrt(HEAD_DIM)
    queries, new_keys, new_values = (part[:, None, :] for part in proj)
    row_at = lax.broadcasted_iota(jnp.int32, (1, HEAD_ROWS, cols), 1)
    lane_at = lax.broadcasted_iota(jnp.int32, (1, HEAD_ROWS, cols), 2)
    head_mask = (lane_at // HEAD_DIM == row_at).astype(jnp.float32)
    spread = queries * head_mask
    scores = batched(spread.astype(jnp.bfloat16), key_cache[...], ((2,), (2,))) * score_scale
    own_score = jnp.sum(spread * new_keys, axis=-1, keepdims=True) * score_scale
    positions = lax.broadcasted_iota(jnp.int32, (slots, HEAD_ROWS, context), 2).astype(jnp.float32)
    limit = jnp.broadcast_to(lengths, (slots, context))[:, None, :]
    scores = jnp.where(positions < limit, scores, -jnp.inf)
    peak = jnp.maximum(jnp.max(scores, axis=-1, keepdims=True), own_score)
    cache_weight = jnp.exp(scores - peak)
    own_weight = jnp.exp(own_score - peak)
    denominator = jnp.sum(cache_weight, axis=-1, keepdims=True) + own_weight
    cache_prob = (cache_weight / denominator).astype(jnp.bfloat16)
    own_prob = (own_weight / denominator).astype(jnp.bfloat16).astype(jnp.float32)
    attended = batched(cache_prob, value_cache[...], ((2,), (1,))) + own_prob * new_values
    return jnp.sum(attended * head_mask, axis=1).astype(jnp.bfloat16)


def kernel(
    req_count,
    head_count,
    deal_ref,
    length_ref,
    routes_ref,
    gates_ref,
    tok_ref,
    again_ref,
    fgain_ref,
    wqkv_hbm,
    key_hbm,
    value_hbm,
    wout_hbm,
    wgate_hbm,
    wup_hbm,
    wdown_hbm,
    out_ref,
    wqkv,
    key_cache,
    value_cache,
    wout,
    wgate,
    wup,
    wdown,
    meta_all,
    tok_all,
    stream_in,
    stream,
    part_out,
    part_in,
    rows_all,
    rows_flat,
    hidden,
    terms_out,
    terms_in,
    made,
    place,
    weights,
    carried,
    last,
    load_sem,
    meta_sem,
    tok_sem,
    next_sem,
    head_sem,
    rows_sem,
    terms_sem,
    made_sem,
    last_sem,
):
    sec = lax.axis_index("section")
    req = lax.axis_index("req")
    head = lax.axis_index("head")
    count = req_count * head_count
    me = req * head_count + head
    slots, width = tok_ref.shape
    own_rows = slots // head_count
    reqs = slots * req_count
    units = wgate.shape[1]
    chunk = 256 if units % 256 == 0 else units

    loads = [
        pltpu.make_async_copy(src.at[0], dst, load_sem.at[i])
        for i, (src, dst) in enumerate(
            [
                (key_hbm, key_cache),
                (value_hbm, value_cache),
                (wout_hbm, wout),
                (wgate_hbm, wgate),
                (wup_hbm, wup),
                (wdown_hbm, wdown),
            ]
        )
    ]
    load_qkv = pltpu.make_async_copy(wqkv_hbm, wqkv, load_sem.at[6])
    load_qkv.start()
    for load in loads:
        load.start()

    def peer_of(k):
        peer = lax.rem(me + k, count)
        return peer, (sec, peer // head_count, lax.rem(peer, head_count))

    def req_peer(k):
        return (sec, lax.rem(req + k, req_count), head)

    def head_peer(k):
        other = lax.rem(head + k, head_count)
        return other, (sec, req, other)

    def each(first, last, body):
        def step(k, carry):
            body(k)
            return carry

        if last - first <= 16:
            for k in range(first, last):
                body(k)
        else:
            lax.fori_loop(first, last, step, 0)

    barrier = pltpu.get_barrier_semaphore()

    def greet(k):
        _, target = peer_of(k)
        pl.semaphore_signal(barrier, inc=1, device_id=target, device_id_type=MESH)

    def greet_other(k):
        pl.semaphore_signal(barrier, inc=1, device_id=(1 - sec, req, k), device_id_type=MESH)

    each(1, count, greet)
    each(0, head_count, greet_other)
    pl.semaphore_wait(barrier, count - 1 + head_count)

    def remote(src, dst, sems, k, target):
        return pltpu.make_async_remote_copy(
            src_ref=src,
            dst_ref=dst,
            send_sem=sems.at[0, k],
            recv_sem=sems.at[1, k],
            device_id=target,
            device_id_type=MESH,
        )

    def meta_copy(k):
        return remote(meta_all.at[req], meta_all.at[req], meta_sem, k, req_peer(k))

    def tok_copy(k):
        return remote(tok_ref, tok_all.at[req], tok_sem, k, req_peer(k))

    def next_copy(k):
        return pltpu.make_async_remote_copy(
            src_ref=made.at[me],
            dst_ref=stream_in.at[head],
            send_sem=next_sem.at[0, k],
            recv_sem=next_sem.at[1, head],
            device_id=(1, req, k),
            device_id_type=MESH,
        )

    def next_arrival(k):
        return pltpu.make_async_remote_copy(
            src_ref=made.at[me],
            dst_ref=stream_in.at[k],
            send_sem=next_sem.at[0, k],
            recv_sem=next_sem.at[1, k],
            device_id=(0, req, k),
            device_id_type=MESH,
        )

    def head_copy(k):
        other, target = head_peer(k)
        return remote(part_out.at[other], part_in.at[head], head_sem, k, target)

    def rows_copy(k):
        _, target = peer_of(k)
        return remote(rows_all.at[me], rows_all.at[me], rows_sem, k, target)

    def terms_copy(k, part):
        peer, target = peer_of(k)
        at = pl.ds(part * (width // PARTS), width // PARTS)
        return remote(
            terms_out.at[peer, :, at],
            terms_in.at[me, :, at],
            terms_sem,
            part * count + k,
            target,
        )

    def made_copy(k):
        _, target = peer_of(k)
        return remote(made.at[me], made.at[me], made_sem, k, target)

    def last_copy(k):
        _, target = head_peer(k)
        return remote(last.at[head], last.at[head], last_sem, k, target)

    @pl.when(sec == 0)
    def _():
        each(1, req_count, lambda k: tok_copy(k).start())

    deal = column(deal_ref[...].astype(jnp.float32))
    lengths = column(length_ref[...].astype(jnp.float32))
    lanes = lax.broadcasted_iota(jnp.int32, (slots, LANES), 1).astype(jnp.float32)
    meta = jnp.where(lanes == DEAL_LANE, deal, 0.0)
    for k in range(routes_ref.shape[0]):
        named = column(routes_ref[k : k + 1, :].astype(jnp.float32))
        weight = column(gates_ref[...].astype(jnp.float32)[k : k + 1, :])
        meta = meta + jnp.where(lanes == named, weight, 0.0)
    meta_all[req] = meta
    each(1, req_count, lambda k: meta_copy(k).start())

    @pl.when(sec == 0)
    def _():
        tok_all[req] = tok_ref[...]
        each(1, req_count, lambda k: tok_copy(k).wait())
        taken = lax.broadcasted_iota(jnp.int32, (slots, reqs), 1) == deal.astype(jnp.int32)
        dealt = jnp.dot(
            taken.astype(jnp.float32).astype(jnp.bfloat16),
            tok_all[...].reshape(reqs, width),
            preferred_element_type=jnp.float32,
        )
        stream[...] = dealt.reshape(head_count, own_rows, width)

    @pl.when(sec == 1)
    def _():
        each(0, head_count, lambda k: next_arrival(k).wait_recv())
        stream[...] = stream_in[...].astype(jnp.float32)

    normed = rms_scale(stream[...].reshape(slots, width), again_ref[...]).astype(jnp.bfloat16)
    load_qkv.wait()
    proj = [
        jnp.dot(normed, wqkv[i], preferred_element_type=jnp.float32)
        .astype(jnp.bfloat16)
        .astype(jnp.float32)
        for i in range(3)
    ]
    for load in loads[:3]:
        load.wait()
    attended = attend(proj, lengths, key_cache, value_cache)
    partial_value = jnp.dot(attended, wout[...], preferred_element_type=jnp.float32)
    part_out[...] = partial_value.reshape(head_count, own_rows, width)
    each(1, head_count, lambda k: head_copy(k).start())
    part_in[head] = part_out[head]
    each(1, head_count, lambda k: head_copy(k).wait())
    residual = stream[head] + jnp.sum(part_in[...], axis=0)
    rows_all[me] = rms_scale(residual, fgain_ref[...]).astype(jnp.bfloat16)
    each(1, count, lambda k: rows_copy(k).start())
    each(1, req_count, lambda k: meta_copy(k).wait())
    lane_at = lax.broadcasted_iota(jnp.int32, (reqs, LANES), 1)
    meta_rows = meta_all[...].reshape(reqs, LANES)
    deal_all = meta_rows[:, DEAL_LANE : DEAL_LANE + 1].astype(jnp.int32)

    @pl.when(sec == 0)
    def _():
        weights[...] = meta_rows

    @pl.when(sec == 1)
    def _():
        slot_to = deal_all == lax.broadcasted_iota(jnp.int32, (reqs, reqs), 1)
        place[...] = slot_to.astype(jnp.float32).reshape(count, own_rows, reqs)
        weights[...] = gathered(
            place[...].reshape(reqs, reqs), meta_rows.astype(jnp.bfloat16)
        )
        high = residual.astype(jnp.bfloat16)
        rest = residual - high.astype(jnp.float32)
        middle = rest.astype(jnp.bfloat16)
        low = (rest - middle.astype(jnp.float32)).astype(jnp.bfloat16)
        mine = place[me]
        carried[...] = gathered(mine, high) + gathered(mine, middle) + gathered(mine, low)

    row_weight = jnp.sum(
        jnp.where(lane_at == me * units // FF, weights[...], 0.0), axis=1, keepdims=True
    )
    each(1, count, lambda k: rows_copy(k).wait())

    @pl.when(sec == 0)
    def _():
        rows_flat[...] = flat(rows_all)

    @pl.when(sec == 1)
    def _():
        rows_flat[...] = gathered(place[...].reshape(reqs, reqs), flat(rows_all)).astype(
            jnp.bfloat16
        )

    for load in loads[3:]:
        load.wait()

    def hide(c):
        at = pl.ds(c * chunk, chunk)
        rows = rows_flat[...]
        gate_part = jnp.dot(rows, wgate[:, at], preferred_element_type=jnp.float32)
        up_part = jnp.dot(rows, wup[:, at], preferred_element_type=jnp.float32)
        hidden[:, at] = (row_weight * gelu(gate_part) * up_part).astype(jnp.bfloat16)

    for c in range(units // chunk):
        hide(c)
    for part in range(PARTS):
        at = pl.ds(part * (width // PARTS), width // PARTS)
        done = jnp.dot(hidden[...], wdown[:, at], preferred_element_type=jnp.float32)

        @pl.when(sec == 0)
        def _():
            terms_out[:, :, at] = done.reshape(count, own_rows, -1).astype(jnp.bfloat16)

        @pl.when(sec == 1)
        def _():
            with_residual = done + carried[:, at]
            terms_out[:, :, at] = with_residual.reshape(count, own_rows, -1).astype(jnp.bfloat16)

        each(1, count, lambda k: terms_copy(k, part).start())
    terms_in[me] = terms_out[me]
    for part in range(PARTS):
        each(1, count, lambda k: terms_copy(k, part).wait())
    mixture = jnp.sum(terms_in[...].astype(jnp.float32), axis=0)

    @pl.when(sec == 0)
    def _():
        made[me] = (residual + mixture).astype(jnp.bfloat16)
        each(0, head_count, lambda k: next_copy(k).start())
        each(1, count, lambda k: made_copy(k).start())
        each(1, count, lambda k: made_copy(k).wait())
        placed = deal_all == req * slots + lax.broadcasted_iota(jnp.int32, (reqs, slots), 1)
        out_ref[...] = gathered(placed.astype(jnp.float32), flat(made))
        each(0, head_count, lambda k: next_copy(k).wait_send())

    @pl.when(sec == 1)
    def _():
        last[head] = mixture.astype(jnp.bfloat16)
        each(1, head_count, lambda k: last_copy(k).start())
        each(1, head_count, lambda k: last_copy(k).wait())
        out_ref[...] = last[...].astype(jnp.float32).reshape(slots, width)


def on_device(
    tokens,
    deal,
    lengths,
    cache_keys,
    cache_values,
    w_qkv,
    w_out,
    attn_gain,
    ffn_gain,
    w_gate,
    w_up,
    w_down,
    routes,
    gates,
):
    req_count = lax.axis_size("req")
    head_count = lax.axis_size("head")
    count = req_count * head_count
    slots, width = tokens.shape
    own_rows = slots // head_count
    reqs = slots * req_count
    units = w_gate.shape[2]
    cols = w_out.shape[1]
    context = cache_keys.shape[2]
    qkv_weight = w_qkv[0].transpose(1, 0, 2)
    bf16, f32 = jnp.bfloat16, jnp.float32
    vmem = pl.BlockSpec(memory_space=pltpu.VMEM)
    anywhere = pl.BlockSpec(memory_space=pl.ANY)

    def sems(n):
        return pltpu.SemaphoreType.DMA((2, n))

    out = pl.pallas_call(
        functools.partial(kernel, req_count, head_count),
        out_shape=jax.ShapeDtypeStruct((slots, width), f32),
        in_specs=[vmem] * 7 + [anywhere] * 7,
        out_specs=vmem,
        scratch_shapes=[
            pltpu.VMEM((3, width, cols), bf16),
            pltpu.VMEM((slots, context, cols), bf16),
            pltpu.VMEM((slots, context, cols), bf16),
            pltpu.VMEM((cols, width), bf16),
            pltpu.VMEM((width, units), bf16),
            pltpu.VMEM((width, units), bf16),
            pltpu.VMEM((units, width), bf16),
            pltpu.VMEM((req_count, slots, LANES), f32),
            pltpu.VMEM((req_count, slots, width), bf16),
            pltpu.VMEM((head_count, own_rows, width), bf16),
            pltpu.VMEM((head_count, own_rows, width), f32),
            pltpu.VMEM((head_count, own_rows, width), f32),
            pltpu.VMEM((head_count, own_rows, width), f32),
            pltpu.VMEM((count, own_rows, width), bf16),
            pltpu.VMEM((reqs, width), bf16),
            pltpu.VMEM((reqs, units), bf16),
            pltpu.VMEM((count, own_rows, width), bf16),
            pltpu.VMEM((count, own_rows, width), bf16),
            pltpu.VMEM((count, own_rows, width), bf16),
            pltpu.VMEM((count, own_rows, reqs), f32),
            pltpu.VMEM((reqs, LANES), f32),
            pltpu.VMEM((reqs, width), f32),
            pltpu.VMEM((head_count, own_rows, width), bf16),
            pltpu.SemaphoreType.DMA((7,)),
            sems(req_count),
            sems(req_count),
            sems(head_count),
            sems(head_count),
            sems(count),
            sems(PARTS * count),
            sems(count),
            sems(head_count),
        ],
        compiler_params=pltpu.CompilerParams(
            collective_id=0, has_side_effects=True, vmem_limit_bytes=56 * 1024 * 1024
        ),
    )(
        deal[None],
        lengths,
        routes[0].T,
        gates[0].T,
        tokens,
        attn_gain,
        ffn_gain,
        qkv_weight,
        cache_keys,
        cache_values,
        w_out,
        w_gate,
        w_up,
        w_down,
    )
    return out.astype(bf16)[None]


def solution(mesh):
    return jax.shard_map(
        on_device,
        mesh=mesh,
        in_specs=(
            P("req", None),
            P("req"),
            P("section", "req"),
            P("section", "req", None, "head"),
            P("section", "req", None, "head"),
            P("section", None, None, "head"),
            P("section", "head", None),
            P("section", None),
            P("section", None),
            P("section", None, ("req", "head")),
            P("section", None, ("req", "head")),
            P("section", ("req", "head"), None),
            P("section", "req", None),
            P("section", "req", None),
        ),
        out_specs=P("section", "req", None),
        check_vma=False,
    )
```

```python
import functools
import math

import jax
import jax.numpy as jnp
from jax import lax
from jax.experimental import pallas as pl
from jax.experimental.pallas import tpu as pltpu
from jax.sharding import PartitionSpec as P

HEAD_DIM = 64
EXPERTS = 16
FF = 2816
LANES = 128
DEAL_LANE = EXPERTS
HEAD_ROWS = 16
PARTS = 2
MESH = pl.DeviceIdType.MESH


epsilon = 1e-06


def rms_scale(values, gain_row):
    mean_square = jnp.mean(values * values, axis=-1, keepdims=True)
    return values * lax.rsqrt(mean_square + epsilon) * gain_row


def column(row):
    size = row.shape[1]
    diagonal = lax.broadcasted_iota(jnp.int32, (size, size), 0) == lax.broadcasted_iota(
        jnp.int32, (size, size), 1
    )
    return jnp.sum(jnp.where(diagonal, row, 0.0), axis=1, keepdims=True)


def gathered(chosen, values):
    return lax.dot_general(
        chosen.astype(jnp.bfloat16),
        values,
        (((0,), (0,)), ((), ())),
        preferred_element_type=jnp.float32,
    )


def flat(blocks):
    count, rows, width = blocks.shape
    return blocks[...].astype(jnp.float32).reshape(count * rows, width).astype(jnp.bfloat16)


def gelu(v):
    return 0.5 * v * (1.0 + jnp.tanh(math.sqrt(2.0 / math.pi) * (v + 0.044715 * (v * v * v))))


def batched(a, b, dims):
    return lax.dot_general(a, b, (dims, ((0,), (0,))), preferred_element_type=jnp.float32)


def attend(proj, lengths, key_cache, value_cache):
    slots, context, cols = key_cache.shape
    score_scale = 1.0 / math.sqrt(HEAD_DIM)
    queries, new_keys, new_values = (part[:, None, :] for part in proj)
    row_at = lax.broadcasted_iota(jnp.int32, (1, HEAD_ROWS, cols), 1)
    lane_at = lax.broadcasted_iota(jnp.int32, (1, HEAD_ROWS, cols), 2)
    head_mask = (lane_at // HEAD_DIM == row_at).astype(jnp.float32)
    spread = queries * head_mask
    scores = batched(spread.astype(jnp.bfloat16), key_cache[...], ((2,), (2,))) * score_scale
    own_score = jnp.sum(spread * new_keys, axis=-1, keepdims=True) * score_scale
    positions = lax.broadcasted_iota(jnp.int32, (slots, HEAD_ROWS, context), 2).astype(jnp.float32)
    limit = jnp.broadcast_to(lengths, (slots, context))[:, None, :]
    scores = jnp.where(positions < limit, scores, -jnp.inf)
    peak = jnp.maximum(jnp.max(scores, axis=-1, keepdims=True), own_score)
    cache_weight = jnp.exp(scores - peak)
    own_weight = jnp.exp(own_score - peak)
    denominator = jnp.sum(cache_weight, axis=-1, keepdims=True) + own_weight
    cache_prob = (cache_weight / denominator).astype(jnp.bfloat16)
    own_prob = (own_weight / denominator).astype(jnp.bfloat16).astype(jnp.float32)
    attended = batched(cache_prob, value_cache[...], ((2,), (1,))) + own_prob * new_values
    return jnp.sum(attended * head_mask, axis=1).astype(jnp.bfloat16)


def kernel(
    req_count,
    head_count,
    deal_ref,
    length_ref,
    routes_ref,
    gates_ref,
    tok_ref,
    again_ref,
    fgain_ref,
    wqkv_hbm,
    key_hbm,
    value_hbm,
    wout_hbm,
    wgate_hbm,
    wup_hbm,
    wdown_hbm,
    out_ref,
    wqkv,
    key_cache,
    value_cache,
    wout,
    wgate,
    wup,
    wdown,
    meta_all,
    tok_all,
    stream_in,
    stream,
    part_out,
    part_in,
    rows_all,
    rows_flat,
    hidden,
    terms_out,
    terms_in,
    made,
    place,
    weights,
    carried,
    last,
    load_sem,
    meta_sem,
    tok_sem,
    next_sem,
    head_sem,
    rows_sem,
    terms_sem,
    made_sem,
    last_sem,
):
    sec = lax.axis_index("section")
    req = lax.axis_index("req")
    head = lax.axis_index("head")
    count = req_count * head_count
    me = req * head_count + head
    slots, width = tok_ref.shape
    own_rows = slots // head_count
    reqs = slots * req_count
    units = wgate.shape[1]
    chunk = 256 if units % 256 == 0 else units

    loads = [
        pltpu.make_async_copy(src.at[0], dst, load_sem.at[i])
        for i, (src, dst) in enumerate(
            [
                (key_hbm, key_cache),
                (value_hbm, value_cache),
                (wout_hbm, wout),
                (wgate_hbm, wgate),
                (wup_hbm, wup),
                (wdown_hbm, wdown),
            ]
        )
    ]
    load_qkv = pltpu.make_async_copy(wqkv_hbm, wqkv, load_sem.at[6])
    load_qkv.start()
    for load in loads:
        load.start()

    def peer_of(k):
        peer = lax.rem(me + k, count)
        return peer, (sec, peer // head_count, lax.rem(peer, head_count))

    def req_peer(k):
        return (sec, lax.rem(req + k, req_count), head)

    def head_peer(k):
        other = lax.rem(head + k, head_count)
        return other, (sec, req, other)

    def each(first, last, body):
        def step(k, carry):
            body(k)
            return carry

        if last - first <= 16:
            for k in range(first, last):
                body(k)
        else:
            lax.fori_loop(first, last, step, 0)

    barrier = pltpu.get_barrier_semaphore()

    def greet(k):
        _, target = peer_of(k)
        pl.semaphore_signal(barrier, inc=1, device_id=target, device_id_type=MESH)

    def greet_other(k):
        pl.semaphore_signal(barrier, inc=1, device_id=(1 - sec, req, k), device_id_type=MESH)

    each(1, count, greet)
    each(0, head_count, greet_other)
    pl.semaphore_wait(barrier, count - 1 + head_count)

    def remote(src, dst, sems, k, target):
        return pltpu.make_async_remote_copy(
            src_ref=src,
            dst_ref=dst,
            send_sem=sems.at[0, k],
            recv_sem=sems.at[1, k],
            device_id=target,
            device_id_type=MESH,
        )

    def meta_copy(k):
        return remote(meta_all.at[req], meta_all.at[req], meta_sem, k, req_peer(k))

    def tok_copy(k):
        return remote(tok_ref, tok_all.at[req], tok_sem, k, req_peer(k))

    def next_copy(k):
        return pltpu.make_async_remote_copy(
            src_ref=made.at[me],
            dst_ref=stream_in.at[head],
            send_sem=next_sem.at[0, k],
            recv_sem=next_sem.at[1, head],
            device_id=(1, req, k),
            device_id_type=MESH,
        )

    def next_arrival(k):
        return pltpu.make_async_remote_copy(
            src_ref=made.at[me],
            dst_ref=stream_in.at[k],
            send_sem=next_sem.at[0, k],
            recv_sem=next_sem.at[1, k],
            device_id=(0, req, k),
            device_id_type=MESH,
        )

    def head_copy(k):
        other, target = head_peer(k)
        return remote(part_out.at[other], part_in.at[head], head_sem, k, target)

    def rows_copy(k):
        _, target = peer_of(k)
        return remote(rows_all.at[me], rows_all.at[me], rows_sem, k, target)

    def terms_copy(k, part):
        peer, target = peer_of(k)
        at = pl.ds(part * (width // PARTS), width // PARTS)
        return remote(
            terms_out.at[peer, :, at],
            terms_in.at[me, :, at],
            terms_sem,
            part * count + k,
            target,
        )

    def made_copy(k):
        _, target = peer_of(k)
        return remote(made.at[me], made.at[me], made_sem, k, target)

    def last_copy(k):
        _, target = head_peer(k)
        return remote(last.at[head], last.at[head], last_sem, k, target)

    @pl.when(sec == 0)
    def _():
        each(1, req_count, lambda k: tok_copy(k).start())

    deal = column(deal_ref[...].astype(jnp.float32))
    lengths = column(length_ref[...].astype(jnp.float32))
    lanes = lax.broadcasted_iota(jnp.int32, (slots, LANES), 1).astype(jnp.float32)
    meta = jnp.where(lanes == DEAL_LANE, deal, 0.0)
    for k in range(routes_ref.shape[0]):
        named = column(routes_ref[k : k + 1, :].astype(jnp.float32))
        weight = column(gates_ref[...].astype(jnp.float32)[k : k + 1, :])
        meta = meta + jnp.where(lanes == named, weight, 0.0)
    meta_all[req] = meta
    each(1, req_count, lambda k: meta_copy(k).start())

    @pl.when(sec == 0)
    def _():
        tok_all[req] = tok_ref[...]
        each(1, req_count, lambda k: tok_copy(k).wait())
        taken = lax.broadcasted_iota(jnp.int32, (slots, reqs), 1) == deal.astype(jnp.int32)
        dealt = jnp.dot(
            taken.astype(jnp.float32).astype(jnp.bfloat16),
            tok_all[...].reshape(reqs, width),
            preferred_element_type=jnp.float32,
        )
        stream[...] = dealt.reshape(head_count, own_rows, width)

    @pl.when(sec == 1)
    def _():
        each(0, head_count, lambda k: next_arrival(k).wait_recv())
        stream[...] = stream_in[...].astype(jnp.float32)

    normed = rms_scale(stream[...].reshape(slots, width), again_ref[...]).astype(jnp.bfloat16)
    load_qkv.wait()
    proj = [
        jnp.dot(normed, wqkv[i], preferred_element_type=jnp.float32)
        .astype(jnp.bfloat16)
        .astype(jnp.float32)
        for i in range(3)
    ]
    for load in loads[:3]:
        load.wait()
    attended = attend(proj, lengths, key_cache, value_cache)
    partial_value = jnp.dot(attended, wout[...], preferred_element_type=jnp.float32)
    part_out[...] = partial_value.reshape(head_count, own_rows, width)
    each(1, head_count, lambda k: head_copy(k).start())
    part_in[head] = part_out[head]
    each(1, head_count, lambda k: head_copy(k).wait())
    residual = stream[head] + jnp.sum(part_in[...], axis=0)
    rows_all[me] = rms_scale(residual, fgain_ref[...]).astype(jnp.bfloat16)
    each(1, count, lambda k: rows_copy(k).start())
    each(1, req_count, lambda k: meta_copy(k).wait())
    lane_at = lax.broadcasted_iota(jnp.int32, (reqs, LANES), 1)
    meta_rows = meta_all[...].reshape(reqs, LANES)
    deal_all = meta_rows[:, DEAL_LANE : DEAL_LANE + 1].astype(jnp.int32)

    @pl.when(sec == 0)
    def _():
        weights[...] = meta_rows

    @pl.when(sec == 1)
    def _():
        slot_to = deal_all == lax.broadcasted_iota(jnp.int32, (reqs, reqs), 1)
        place[...] = slot_to.astype(jnp.float32).reshape(count, own_rows, reqs)
        weights[...] = gathered(
            place[...].reshape(reqs, reqs), meta_rows.astype(jnp.bfloat16)
        )
        high = residual.astype(jnp.bfloat16)
        rest = residual - high.astype(jnp.float32)
        middle = rest.astype(jnp.bfloat16)
        low = (rest - middle.astype(jnp.float32)).astype(jnp.bfloat16)
        mine = place[me]
        carried[...] = gathered(mine, high) + gathered(mine, middle) + gathered(mine, low)

    row_weight = jnp.sum(
        jnp.where(lane_at == me * units // FF, weights[...], 0.0), axis=1, keepdims=True
    )
    each(1, count, lambda k: rows_copy(k).wait())

    @pl.when(sec == 0)
    def _():
        rows_flat[...] = flat(rows_all)

    @pl.when(sec == 1)
    def _():
        rows_flat[...] = gathered(place[...].reshape(reqs, reqs), flat(rows_all)).astype(
            jnp.bfloat16
        )

    for load in loads[3:]:
        load.wait()

    def hide(c):
        at = pl.ds(c * chunk, chunk)
        rows = rows_flat[...]
        gate_part = jnp.dot(rows, wgate[:, at], preferred_element_type=jnp.float32)
        up_part = jnp.dot(rows, wup[:, at], preferred_element_type=jnp.float32)
        hidden[:, at] = (row_weight * gelu(gate_part) * up_part).astype(jnp.bfloat16)

    for c in range(units // chunk):
        hide(c)
    for part in range(PARTS):
        at = pl.ds(part * (width // PARTS), width // PARTS)
        done = jnp.dot(hidden[...], wdown[:, at], preferred_element_type=jnp.float32)

        @pl.when(sec == 0)
        def _():
            terms_out[:, :, at] = done.reshape(count, own_rows, -1).astype(jnp.bfloat16)

        @pl.when(sec == 1)
        def _():
            with_residual = done + carried[:, at]
            terms_out[:, :, at] = with_residual.reshape(count, own_rows, -1).astype(jnp.bfloat16)

        each(1, count, lambda k: terms_copy(k, part).start())
    terms_in[me] = terms_out[me]
    for part in range(PARTS):
        each(1, count, lambda k: terms_copy(k, part).wait())
    mixture = jnp.sum(terms_in[...].astype(jnp.float32), axis=0)

    @pl.when(sec == 0)
    def _():
        made[me] = (residual + mixture).astype(jnp.bfloat16)
        each(0, head_count, lambda k: next_copy(k).start())
        each(0, head_count, lambda k: next_copy(k).wait_send())
        each(1, count, lambda k: made_copy(k).start())
        each(1, count, lambda k: made_copy(k).wait())
        placed = deal_all == req * slots + lax.broadcasted_iota(jnp.int32, (reqs, slots), 1)
        out_ref[...] = gathered(placed.astype(jnp.float32), flat(made))

    @pl.when(sec == 1)
    def _():
        last[head] = mixture.astype(jnp.bfloat16)
        each(1, head_count, lambda k: last_copy(k).start())
        each(1, head_count, lambda k: last_copy(k).wait())
        out_ref[...] = last[...].astype(jnp.float32).reshape(slots, width)


def on_device(
    tokens,
    deal,
    lengths,
    cache_keys,
    cache_values,
    w_qkv,
    w_out,
    attn_gain,
    ffn_gain,
    w_gate,
    w_up,
    w_down,
    routes,
    gates,
):
    req_count = lax.axis_size("req")
    head_count = lax.axis_size("head")
    count = req_count * head_count
    slots, width = tokens.shape
    own_rows = slots // head_count
    reqs = slots * req_count
    units = w_gate.shape[2]
    cols = w_out.shape[1]
    context = cache_keys.shape[2]
    qkv_weight = w_qkv[0].transpose(1, 0, 2)
    bf16, f32 = jnp.bfloat16, jnp.float32
    vmem = pl.BlockSpec(memory_space=pltpu.VMEM)
    anywhere = pl.BlockSpec(memory_space=pl.ANY)

    def sems(n):
        return pltpu.SemaphoreType.DMA((2, n))

    out = pl.pallas_call(
        functools.partial(kernel, req_count, head_count),
        out_shape=jax.ShapeDtypeStruct((slots, width), f32),
        in_specs=[vmem] * 7 + [anywhere] * 7,
        out_specs=vmem,
        scratch_shapes=[
            pltpu.VMEM((3, width, cols), bf16),
            pltpu.VMEM((slots, context, cols), bf16),
            pltpu.VMEM((slots, context, cols), bf16),
            pltpu.VMEM((cols, width), bf16),
            pltpu.VMEM((width, units), bf16),
            pltpu.VMEM((width, units), bf16),
            pltpu.VMEM((units, width), bf16),
            pltpu.VMEM((req_count, slots, LANES), f32),
            pltpu.VMEM((req_count, slots, width), bf16),
            pltpu.VMEM((head_count, own_rows, width), bf16),
            pltpu.VMEM((head_count, own_rows, width), f32),
            pltpu.VMEM((head_count, own_rows, width), f32),
            pltpu.VMEM((head_count, own_rows, width), f32),
            pltpu.VMEM((count, own_rows, width), bf16),
            pltpu.VMEM((reqs, width), bf16),
            pltpu.VMEM((reqs, units), bf16),
            pltpu.VMEM((count, own_rows, width), bf16),
            pltpu.VMEM((count, own_rows, width), bf16),
            pltpu.VMEM((count, own_rows, width), bf16),
            pltpu.VMEM((count, own_rows, reqs), f32),
            pltpu.VMEM((reqs, LANES), f32),
            pltpu.VMEM((reqs, width), f32),
            pltpu.VMEM((head_count, own_rows, width), bf16),
            pltpu.SemaphoreType.DMA((7,)),
            sems(req_count),
            sems(req_count),
            sems(head_count),
            sems(head_count),
            sems(count),
            sems(PARTS * count),
            sems(count),
            sems(head_count),
        ],
        compiler_params=pltpu.CompilerParams(
            collective_id=0, has_side_effects=True, vmem_limit_bytes=56 * 1024 * 1024
        ),
    )(
        deal[None],
        lengths,
        routes[0].T,
        gates[0].T,
        tokens,
        attn_gain,
        ffn_gain,
        qkv_weight,
        cache_keys,
        cache_values,
        w_out,
        w_gate,
        w_up,
        w_down,
    )
    return out.astype(bf16)[None]


def solution(mesh):
    return jax.shard_map(
        on_device,
        mesh=mesh,
        in_specs=(
            P("req", None),
            P("req"),
            P("section", "req"),
            P("section", "req", None, "head"),
            P("section", "req", None, "head"),
            P("section", None, None, "head"),
            P("section", "head", None),
            P("section", None),
            P("section", None),
            P("section", None, ("req", "head")),
            P("section", None, ("req", "head")),
            P("section", ("req", "head"), None),
            P("section", "req", None),
            P("section", "req", None),
        ),
        out_specs=P("section", "req", None),
        check_vma=False,
    )
```
